128 devices in a mesh: gx: 16 (over y, x), yz: 8 (over z, core).
Axes of the slice: x: 4, y: 4, z: 4, core: 2. Of those that a mesh axis runs over, the one named last changes fastest.
Arguments:
- fields: bfloat16 [4, 512, 262144], P(None, 'gx', 'yz'), may hold values from -8 to 8
- test_matrix: float32 [512, 64], replicated, may hold values from -6 to 6
Outputs:
- factor: float32 [512, 64], replicated
- core: bfloat16 [64, 4, 262144], P('gx', None, 'yz')
The draws below stay inside these ranges and needn't reach their ends.
All inputs are finite; a program needn't handle non-finite values.
Results may differ from the reference program's by a relative error of at most 0.0036.
Values may be sent and summed in bfloat16 or wider, within the bound.
No kernel may reach another device: no remote copies, remote signals or barrier semaphores. Data moves between devices by JAX's collectives and lax.ppermute only.
A program may use at most 192 MiB of HBM per device.

```python
import math
import jax
import jax.numpy as jnp
from jax import lax

NX = 512
RANK = 64
SPECIES = 4
CELLS_YZ = 32768
CELLS = 262144


def draw_fields(key, part):
    keys = jax.random.split(jax.random.fold_in(key, 11), 3)
    basis = jax.random.normal(keys[0], (NX, RANK), jnp.float32) / math.sqrt(NX)
    amps = jnp.exp(jax.random.uniform(keys[1], (RANK,), jnp.float32, math.log(0.5), math.log(5.0)))
    region = jnp.arange(CELLS, dtype=jnp.int32) * RANK // CELLS
    bump = 0.3 + 1.5 * (region[None, :] == jnp.arange(RANK, dtype=jnp.int32)[:, None]).astype(jnp.float32)
    weights = amps[:, None] * bump

    def one_species(species_key):
        parts = jax.random.split(species_key, 3)
        level = jax.random.uniform(parts[0], (), jnp.float32, 0.6, 1.4)
        coeff = jax.random.normal(parts[1], (RANK, CELLS), jnp.float32) * weights * level
        noise = 0.5 * jax.random.normal(parts[2], (NX, CELLS), jnp.float32)
        values = jnp.dot(basis, coeff) + noise
        return jnp.clip(values, -8.0, 8.0).astype(jnp.bfloat16)
    return lax.map(one_species, jax.random.split(keys[2], SPECIES))


def scatter_about(stream_key, shape, scale, most, kind=jnp.bfloat16):
    values = scale * jax.random.normal(stream_key, shape, jnp.float32)
    return jnp.clip(values, min=-most, max=most).astype(kind)


def setup_inputs(seed: int = 0) -> dict:
    key_list = jax.random.split(jax.random.key(seed), 3)
    return {
        "fields": draw_fields(jax.random.fold_in(key_list[2], 71), 0),
        "test_matrix": scatter_about(key_list[1], (NX, RANK), 1.0, 6.0, jnp.float32),
    }


def orthonormal(matrix_y):
    moment = jnp.dot(matrix_y.T, matrix_y, precision=lax.Precision.HIGHEST)
    lower = jnp.linalg.cholesky(moment)
    return lax.linalg.triangular_solve(lower, matrix_y, left_side=False, lower=True, transpose_a=True)

def reference(fields, test_matrix):
    block_count = CELLS // CELLS_YZ

    def add_block(index, total):
        first = (index * CELLS_YZ).astype(jnp.int32)
        block = lax.dynamic_slice_in_dim(fields, first, CELLS_YZ, 2)
        for species in range(SPECIES):
            total = total + jnp.dot(block[species].astype(jnp.float32), block[species].T.astype(jnp.float32), preferred_element_type=jnp.float32)
        return total
    gram = lax.fori_loop(0, block_count, add_block, jnp.zeros((NX, NX), jnp.float32))
    sketch = jnp.dot(gram, test_matrix, precision=lax.Precision.HIGHEST) / (SPECIES * CELLS)
    factor = orthonormal(orthonormal(sketch))
    factor_low = factor.astype(jnp.bfloat16)

    def core_block(index):
        first = (index * CELLS_YZ).astype(jnp.int32)
        block = lax.dynamic_slice_in_dim(fields, first, CELLS_YZ, 2)
        return jnp.stack([jnp.dot(factor_low.T.astype(jnp.float32), block[species].astype(jnp.float32), preferred_element_type=jnp.float32) for species in range(SPECIES)], axis=1)
    blocks = lax.map(core_block, jnp.arange(block_count, dtype=jnp.int32))
    core = jnp.transpose(blocks, (1, 2, 0, 3)).reshape(RANK, SPECIES, CELLS).astype(jnp.bfloat16)
    return (factor, core)
```

```python
import jax
import jax.numpy as jnp
from jax import lax
from jax.sharding import PartitionSpec as P
from jax.experimental import pallas as pl
from jax.experimental.pallas import tpu as pltpu

HIGH = lax.Precision.HIGHEST
F32 = jnp.float32
BF16 = jnp.bfloat16
VM = pl.BlockSpec(memory_space=pltpu.VMEM)
ANY = pl.BlockSpec(memory_space=pl.ANY)


def nt(a, b, precision=None):
    return lax.dot_general(a, b, (((1,), (1,)), ((), ())), precision=precision,
                           preferred_element_type=F32)


def split_kernel(x_ref, o_ref, buf, sem_in, sem_out):
    parts, _, _, w = o_ref.shape

    def load(j):
        return pltpu.make_async_copy(x_ref.at[:, :, pl.ds(j * w, w)], buf.at[j], sem_in.at[j])

    def store(j):
        return pltpu.make_async_copy(buf.at[j], o_ref.at[j], sem_out.at[j])

    for j in range(parts):
        load(j).start()
    for j in range(parts):
        load(j).wait()
        store(j).start()
    for j in range(parts):
        store(j).wait()


def split_cells(fields, parts):
    s, m, n = fields.shape
    shape = (parts, s, m, n // parts)
    return pl.pallas_call(
        split_kernel,
        in_specs=[ANY],
        out_specs=ANY,
        out_shape=jax.ShapeDtypeStruct(shape, fields.dtype),
        scratch_shapes=[pltpu.VMEM(shape, fields.dtype),
                        pltpu.SemaphoreType.DMA((parts,)), pltpu.SemaphoreType.DMA((parts,))],
        compiler_params=pltpu.CompilerParams(vmem_limit_bytes=12 << 20),
        name="split",
    )(fields)


def sketch_kernel(scale, x_ref, t_ref, o_ref, acc):
    k = pl.program_id(0)
    x = x_ref[...].reshape(-1, x_ref.shape[-1])
    g = nt(x, x)

    @pl.when(k == 0)
    def _():
        acc[...] = g

    @pl.when(k > 0)
    def _():
        acc[...] += g

    @pl.when(k == pl.num_programs(0) - 1)
    def _():
        sk = lax.dot_general(t_ref[...], acc[...], (((0,), (0,)), ((), ())), precision=HIGH,
                             preferred_element_type=F32) * scale
        for c in range(4):
            o_ref[c * 64:(c + 1) * 64, :] = sk[:, c * 128:(c + 1) * 128]


def local_sketch(pieces, test_matrix, scale):
    parts, s, m, w = pieces.shape
    return pl.pallas_call(
        lambda *r: sketch_kernel(scale, *r),
        grid=(s,),
        in_specs=[pl.BlockSpec((parts, 1, m, w), lambda k: (0, k, 0, 0)),
                  pl.BlockSpec((512, 64), lambda k: (0, 0))],
        out_specs=pl.BlockSpec((256, 128), lambda k: (0, 0)),
        out_shape=jax.ShapeDtypeStruct((256, 128), F32),
        scratch_shapes=[pltpu.VMEM((512, 512), F32)],
        compiler_params=pltpu.CompilerParams(vmem_limit_bytes=16 << 20),
        name="sketch",
    )(pieces, test_matrix)


def inverse_lower(aug, step):
    blocks = [aug[8 * b:8 * b + 8, :] for b in range(8)]
    sub = lax.broadcasted_iota(jnp.int32, (8, 128), 0)
    for k in range(0, 64, step):
        b0 = k // 8
        cols = [[jnp.broadcast_to(blocks[b][:, 64 + k + j:65 + k + j], (8, 128)) for b in range(b0, 8)]
                for j in range(step)]
        rows = [blocks[b0][k % 8 + j:k % 8 + j + 1, :] for j in range(step)]
        mult = []
        for j in range(step):
            r = k % 8 + j
            inv = 1.0 / cols[j][0][r:r + 1, :]
            l = [c * inv for c in cols[j]]
            l[0] = jnp.where(sub > r, l[0], 0.0)
            for j2 in range(j + 1, step):
                e = cols[j2][0][r:r + 1, :]
                cols[j2] = [c - x * e for c, x in zip(cols[j2], l)]
                rows[j2] = rows[j2] - l[0][r + j2 - j:r + j2 - j + 1, :] * rows[j]
            mult.append(l)
        for b in range(b0, 8):
            t = blocks[b]
            for j in range(step):
                t = t - mult[j][b - b0] * rows[j]
            blocks[b] = t
    lane = lax.broadcasted_iota(jnp.int32, (8, 128), 1)
    out = []
    for b in range(8):
        diag = jnp.sum(jnp.where(lane == sub + 64 + 8 * b, blocks[b], 0.0), axis=1, keepdims=True)
        out.append(blocks[b] * lax.rsqrt(diag))
    return jnp.concatenate(out, axis=0)[:, :64]


def orthonormal_t(yt, step):
    zero = jnp.zeros_like(yt)
    aug = nt(yt, jnp.concatenate([zero, yt], axis=0), HIGH)
    i = lax.broadcasted_iota(jnp.int32, aug.shape, 0)
    j = lax.broadcasted_iota(jnp.int32, aug.shape, 1)
    aug = jnp.where(i == j, 1.0, aug)
    return jnp.dot(inverse_lower(aug, step), yt, precision=HIGH, preferred_element_type=F32)


def core_kernel(y_ref, x_ref, f_ref, o_ref, buf, sem):
    s = x_ref.shape[1]
    w = x_ref.shape[-1]
    loads = [pltpu.make_async_copy(x_ref.at[:, k], buf.at[k], sem.at[k]) for k in range(s)]
    for c in loads:
        c.start()
    yt = jnp.concatenate([y_ref[c * 64:(c + 1) * 64, :] for c in range(4)], axis=1)
    ft = orthonormal_t(orthonormal_t(yt, 4), 4)
    f_ref[...] = ft
    low = ft.astype(BF16)
    i = lax.broadcasted_iota(jnp.int32, (64 * s, 64), 0)
    j = lax.broadcasted_iota(jnp.int32, (64 * s, 64), 1)
    wide = [jnp.dot((i == j * s + k).astype(BF16), low, preferred_element_type=F32).astype(BF16)
            for k in range(s)]
    for c in loads:
        c.wait()
    step = 512
    for c in range(w // step):
        acc = None
        for k in range(s):
            x = buf[k, :, :, c * step:(c + 1) * step].reshape(512, step)
            t = jnp.dot(wide[k], x, preferred_element_type=F32)
            acc = t if acc is None else acc + t
        o_ref[:, :, c * step:(c + 1) * step] = acc.astype(BF16).reshape(16, 4 * s, step)


def core_blocks(full, pieces):
    parts, s, m, w = pieces.shape
    return pl.pallas_call(
        core_kernel,
        in_specs=[VM, ANY],
        out_specs=[VM, VM],
        out_shape=[jax.ShapeDtypeStruct((64, 512), F32),
                   jax.ShapeDtypeStruct((parts, 4 * s, w), BF16)],
        scratch_shapes=[pltpu.VMEM((s, parts, m, w), BF16), pltpu.SemaphoreType.DMA((s,))],
        compiler_params=pltpu.CompilerParams(vmem_limit_bytes=24 << 20),
        name="core",
    )(full, pieces)


def merge_kernel(x_ref, o_ref):
    o_ref[...] = x_ref[0].reshape(o_ref.shape)


def merge_cells(core, s):
    parts, q, w = core.shape
    return pl.pallas_call(
        merge_kernel,
        grid=(parts,),
        in_specs=[pl.BlockSpec((1, q, w), lambda j: (j, 0, 0))],
        out_specs=pl.BlockSpec((q // s, s, w), lambda j: (0, 0, j)),
        out_shape=jax.ShapeDtypeStruct((q // s, s, parts * w), BF16),
        name="merge",
    )(core)


def body(fields, test_matrix):
    s, m, n = fields.shape
    parts = lax.axis_size("gx")
    w = n // parts
    axes = ("gx", "yz")
    scale = 1.0 / (s * n * lax.axis_size("yz"))
    f = split_cells(fields, parts).reshape(parts, s * m, w)
    pieces = lax.all_to_all(f, "gx", split_axis=0, concat_axis=0, tiled=True)
    pieces = pieces.reshape(parts, s, m, w)
    part = local_sketch(pieces, test_matrix, scale)
    part = lax.all_to_all(part.reshape(128, 2, 128), axes, split_axis=0, concat_axis=0, tiled=True)
    part = jnp.sum(part, axis=0, keepdims=True)
    full = lax.all_to_all(jnp.broadcast_to(part, (128, 2, 128)), axes, split_axis=0, concat_axis=0, tiled=True)
    ft, core = core_blocks(full.reshape(256, 128), pieces)
    core = lax.all_to_all(core, "gx", split_axis=0, concat_axis=0, tiled=True)
    return (ft.T, merge_cells(core, s))


def solution(mesh):
    in_specs = (P(None, "gx", "yz"), P())
    out_specs = (P(), P("gx", None, "yz"))
    return jax.shard_map(body, mesh=mesh, in_specs=in_specs, out_specs=out_specs, check_vma=False)
```

```python
import jax
import jax.numpy as jnp
from jax import lax
from jax.sharding import PartitionSpec as P
from jax.experimental import pallas as pl
from jax.experimental.pallas import tpu as pltpu

HIGH = lax.Precision.HIGHEST
F32 = jnp.float32
BF16 = jnp.bfloat16
VM = pl.BlockSpec(memory_space=pltpu.VMEM)
ANY = pl.BlockSpec(memory_space=pl.ANY)


def nt(a, b, precision=None):
    return lax.dot_general(a, b, (((1,), (1,)), ((), ())), precision=precision,
                           preferred_element_type=F32)


def split_kernel(x_ref, o_ref, buf, sem_in, sem_out):
    parts, _, _, w = o_ref.shape

    def load(j):
        return pltpu.make_async_copy(x_ref.at[:, :, pl.ds(j * w, w)], buf.at[j], sem_in.at[j])

    def store(j):
        return pltpu.make_async_copy(buf.at[j], o_ref.at[j], sem_out.at[j])

    for j in range(parts):
        load(j).start()
    for j in range(parts):
        load(j).wait()
        store(j).start()
    for j in range(parts):
        store(j).wait()


def split_cells(fields, parts):
    s, m, n = fields.shape
    shape = (parts, s, m, n // parts)
    return pl.pallas_call(
        split_kernel,
        in_specs=[ANY],
        out_specs=ANY,
        out_shape=jax.ShapeDtypeStruct(shape, fields.dtype),
        scratch_shapes=[pltpu.VMEM(shape, fields.dtype),
                        pltpu.SemaphoreType.DMA((parts,)), pltpu.SemaphoreType.DMA((parts,))],
        compiler_params=pltpu.CompilerParams(vmem_limit_bytes=12 << 20),
        name="split",
    )(fields)


def sketch_kernel(scale, x_ref, t_ref, o_ref):
    parts, s, m, w = x_ref.shape
    h = parts * m // 2
    gram = [None] * 3
    for k in range(s):
        x = x_ref[:, k].reshape(2 * h, w)
        top, low = x[:h], x[h:]
        for i, (p, q) in enumerate(((top, top), (top, low), (low, low))):
            g = nt(p, q)
            gram[i] = g if k == 0 else gram[i] + g
    gram = jnp.concatenate([jnp.concatenate(gram[:2], axis=1),
                            jnp.concatenate([gram[1].T, gram[2]], axis=1)], axis=0)
    sk = jnp.dot(t_ref[...], gram, precision=HIGH, preferred_element_type=F32) * scale
    for c in range(4):
        o_ref[c * 64:(c + 1) * 64, :] = sk[:, c * 128:(c + 1) * 128]


def local_sketch(pieces, test_t, scale):
    return pl.pallas_call(
        lambda *r: sketch_kernel(scale, *r),
        in_specs=[VM, VM],
        out_specs=VM,
        out_shape=jax.ShapeDtypeStruct((256, 128), F32),
        compiler_params=pltpu.CompilerParams(vmem_limit_bytes=24 << 20),
        name="sketch",
    )(pieces, test_t)


def total_kernel(x_ref, o_ref):
    y = jnp.sum(x_ref[...].reshape(-1, 8, 128), axis=0)
    y = y + pltpu.roll(y, 4, 0)
    y = y + pltpu.roll(y, 2, 0)
    o_ref[...] = jnp.broadcast_to(y[None], (32, 8, 128)).reshape(256, 128)


def total(part):
    return pl.pallas_call(
        total_kernel,
        in_specs=[VM],
        out_specs=VM,
        out_shape=jax.ShapeDtypeStruct((256, 128), F32),
        compiler_params=pltpu.CompilerParams(vmem_limit_bytes=2 << 20),
        name="total",
    )(part)


def inverse_lower(aug, step):
    blocks = [aug[8 * b:8 * b + 8, :] for b in range(8)]
    sub = lax.broadcasted_iota(jnp.int32, (8, 128), 0)
    for k in range(0, 64, step):
        b0 = k // 8
        cols = [[jnp.broadcast_to(blocks[b][:, 64 + k + j:65 + k + j], (8, 128)) for b in range(b0, 8)]
                for j in range(step)]
        rows = [blocks[b0][k % 8 + j:k % 8 + j + 1, :] for j in range(step)]
        mult = []
        for j in range(step):
            r = k % 8 + j
            inv = 1.0 / cols[j][0][r:r + 1, :]
            l = [c * inv for c in cols[j]]
            l[0] = jnp.where(sub > r, l[0], 0.0)
            for j2 in range(j + 1, step):
                e = cols[j2][0][r:r + 1, :]
                cols[j2] = [c - x * e for c, x in zip(cols[j2], l)]
                rows[j2] = rows[j2] - l[0][r + j2 - j:r + j2 - j + 1, :] * rows[j]
            mult.append(l)
        for b in range(b0, 8):
            t = blocks[b]
            for j in range(step):
                t = t - mult[j][b - b0] * rows[j]
            blocks[b] = t
    lane = lax.broadcasted_iota(jnp.int32, (8, 128), 1)
    out = []
    for b in range(8):
        diag = jnp.sum(jnp.where(lane == sub + 64 + 8 * b, blocks[b], 0.0), axis=1, keepdims=True)
        out.append(blocks[b] * lax.rsqrt(diag))
    return jnp.concatenate(out, axis=0)[:, :64]


def orthonormal_t(yt, step):
    zero = jnp.zeros_like(yt)
    aug = nt(yt, jnp.concatenate([zero, yt], axis=0), HIGH)
    i = lax.broadcasted_iota(jnp.int32, aug.shape, 0)
    j = lax.broadcasted_iota(jnp.int32, aug.shape, 1)
    aug = jnp.where(i == j, 1.0, aug)
    return jnp.dot(inverse_lower(aug, step), yt, precision=HIGH, preferred_element_type=F32)


def core_kernel(y_ref, x_ref, f_ref, o_ref):
    parts, s, m, w = x_ref.shape
    yt = jnp.concatenate([y_ref[c * 64:(c + 1) * 64, :] for c in range(4)], axis=1)
    ft = orthonormal_t(orthonormal_t(yt, 4), 4)
    f_ref[...] = ft
    low = ft.astype(BF16)
    i = lax.broadcasted_iota(jnp.int32, (64 * s, 64), 0)
    j = lax.broadcasted_iota(jnp.int32, (64 * s, 64), 1)
    wide = [jnp.dot((i == j * s + k).astype(BF16), low, preferred_element_type=F32).astype(BF16)
            for k in range(s)]
    step = 512
    for c in range(w // step):
        acc = None
        for k in range(s):
            x = x_ref[:, k, :, c * step:(c + 1) * step].reshape(parts * m, step)
            t = jnp.dot(wide[k], x, preferred_element_type=F32)
            acc = t if acc is None else acc + t
        o_ref[:, :, :, c * step:(c + 1) * step] = acc.astype(BF16).reshape(o_ref.shape[:3] + (step,))


def core_blocks(full, pieces):
    parts, s, m, w = pieces.shape
    return pl.pallas_call(
        core_kernel,
        in_specs=[VM, VM],
        out_specs=[VM, VM],
        out_shape=[jax.ShapeDtypeStruct((64, 512), F32),
                   jax.ShapeDtypeStruct((parts, 64 // parts, s, w), BF16)],
        compiler_params=pltpu.CompilerParams(vmem_limit_bytes=24 << 20),
        name="core",
    )(full, pieces)


def merge_kernel(x_ref, o_ref, sem):
    parts, _, _, w = x_ref.shape
    copies = [pltpu.make_async_copy(x_ref.at[j], o_ref.at[:, :, pl.ds(j * w, w)], sem.at[j])
              for j in range(parts)]
    for c in copies:
        c.start()
    for c in copies:
        c.wait()


def merge_cells(core):
    parts, q, s, w = core.shape
    return pl.pallas_call(
        merge_kernel,
        in_specs=[VM],
        out_specs=ANY,
        out_shape=jax.ShapeDtypeStruct((q, s, parts * w), BF16),
        scratch_shapes=[pltpu.SemaphoreType.DMA((parts,))],
        compiler_params=pltpu.CompilerParams(vmem_limit_bytes=4 << 20),
        name="merge",
    )(core)


def body(fields, test_matrix):
    s, m, n = fields.shape
    parts = lax.axis_size("gx")
    w = n // parts
    axes = ("gx", "yz")
    scale = 1.0 / (s * n * lax.axis_size("yz"))
    f = split_cells(fields, parts).reshape(parts, s * m, w)
    pieces = lax.all_to_all(f, "gx", split_axis=0, concat_axis=0, tiled=True)
    pieces = pieces.reshape(parts, s, m, w)
    part = local_sketch(pieces, test_matrix.T, scale)
    part = lax.all_to_all(part.reshape(128, 2, 128), axes, split_axis=0, concat_axis=0, tiled=True)
    part = total(part.reshape(256, 128))
    full = lax.all_to_all(part.reshape(128, 2, 128), axes, split_axis=0, concat_axis=0, tiled=True)
    ft, core = core_blocks(full.reshape(256, 128), pieces)
    core = lax.all_to_all(core, "gx", split_axis=0, concat_axis=0, tiled=True)
    return (ft.T, merge_cells(core))


def solution(mesh):
    in_specs = (P(None, "gx", "yz"), P())
    out_specs = (P(), P("gx", None, "yz"))
    return jax.shard_map(body, mesh=mesh, in_specs=in_specs, out_specs=out_specs, check_vma=False)
```

```python
import jax
import jax.numpy as jnp
from jax import lax
from jax.sharding import PartitionSpec as P
from jax.experimental import pallas as pl
from jax.experimental.pallas import tpu as pltpu

HIGH = lax.Precision.HIGHEST
F32 = jnp.float32
BF16 = jnp.bfloat16
VM = pl.BlockSpec(memory_space=pltpu.VMEM)
ANY = pl.BlockSpec(memory_space=pl.ANY)


def nt(a, b, precision=None):
    return lax.dot_general(a, b, (((1,), (1,)), ((), ())), precision=precision,
                           preferred_element_type=F32)


def place():
    g = lax.axis_index("gx")
    return lax.rem(g, 4), lax.div(g, 4)


def member(x, y):
    return lax.rem(y + 4, 4) * 4 + lax.rem(x + 4, 4)


def split_kernel(x_ref, *outs):
    w = outs[0].shape[-1]
    x, y = place()
    for k in range(2):
        for d in range(4):
            for q in range(4):
                j = member(x + q, y + d) if k else member(x + d, y + q)
                outs[4 * k + d][q] = x_ref[k, :, pl.ds(pl.multiple_of(j * w, w), w)]


def split_pair(pair, parts):
    _, m, n = pair.shape
    out = jax.ShapeDtypeStruct((4, m, n // parts), pair.dtype)
    outs = pl.pallas_call(
        split_kernel,
        in_specs=[VM],
        out_specs=[VM] * 8,
        out_shape=[out] * 8,
        compiler_params=pltpu.CompilerParams(vmem_limit_bytes=10 << 20),
        cost_estimate=pl.CostEstimate(flops=0, transcendentals=0, bytes_accessed=8 * m * n),
        name="split",
    )(pair)
    return list(outs[:4]), list(outs[4:])


def shift(v, along, d):
    step = 1 if along == "x" else 4
    pairs = []
    for g in range(16):
        c = (g // step) % 4
        pairs.append((g, g + ((c + d) % 4 - c) * step))
    return lax.ppermute(v, "gx", pairs)


def regroup_kernel(*refs):
    for k in range(2):
        got, out = refs[4 * k:4 * k + 4], refs[8 + 3 * k:11 + 3 * k]
        for q in range(1, 4):
            for d in range(4):
                out[q - 1][d] = got[d][q]


def regroup(one, two):
    out = jax.ShapeDtypeStruct(one[0].shape, one[0].dtype)
    outs = pl.pallas_call(
        regroup_kernel,
        in_specs=[VM] * 8,
        out_specs=[VM] * 6,
        out_shape=[out] * 6,
        compiler_params=pltpu.CompilerParams(vmem_limit_bytes=6 << 20),
        cost_estimate=pl.CostEstimate(flops=0, transcendentals=0, bytes_accessed=4 * out.size),
        name="regroup",
    )(*one, *two)
    return outs[:3], outs[3:]


def gram_kernel(first, scale, *refs):
    blocks, rest = refs[:7], list(refs[7:])
    acc = rest.pop(0) if len(rest) > 2 else None
    t_ref = rest.pop(0) if len(rest) > 2 else None
    p_ref, o_ref = rest
    parts, m, w = p_ref.shape
    x, y = place()
    for d1 in range(4):
        for d2 in range(4):
            g = member(x - d1, y - d2) if first == "x" else member(x - d2, y - d1)
            p_ref[g] = blocks[d1][0] if d2 == 0 else blocks[3 + d2][d1]
    h = parts * m // 2
    top = p_ref[:parts // 2].reshape(h, w)
    low = p_ref[parts // 2:].reshape(h, w)
    gram = [nt(p, q) for p, q in ((top, top), (top, low), (low, low))]
    if acc is not None:
        gram = [g + acc[k] for k, g in enumerate(gram)]
    if t_ref is None:
        for k in range(3):
            o_ref[k] = gram[k]
        return
    gram = jnp.concatenate([jnp.concatenate(gram[:2], axis=1),
                            jnp.concatenate([gram[1].T, gram[2]], axis=1)], axis=0)
    sk = jnp.dot(t_ref[...], gram, precision=HIGH, preferred_element_type=F32) * scale
    for c in range(4):
        o_ref[c * 64:(c + 1) * 64, :] = sk[:, c * 128:(c + 1) * 128]


def add_gram(first, blocks, acc=None, test_t=None, scale=1.0):
    _, m, w = blocks[0].shape
    args = list(blocks) + [v for v in (acc, test_t) if v is not None]
    shape = (3, 256, 256) if test_t is None else (256, 128)
    return pl.pallas_call(
        lambda *r: gram_kernel(first, scale, *r),
        in_specs=[VM] * len(args),
        out_specs=[VM, VM],
        out_shape=[jax.ShapeDtypeStruct((16, m, w), BF16), jax.ShapeDtypeStruct(shape, F32)],
        compiler_params=pltpu.CompilerParams(vmem_limit_bytes=16 << 20),
        cost_estimate=pl.CostEstimate(flops=3 * 2 * 256 * 256 * w, transcendentals=0,
                                      bytes_accessed=16 * m * w * 4),
        name="gram",
    )(*args)


def total_kernel(x_ref, o_ref):
    y = jnp.sum(x_ref[...].reshape(-1, 8, 128), axis=0)
    y = y + pltpu.roll(y, 4, 0)
    y = y + pltpu.roll(y, 2, 0)
    o_ref[...] = jnp.broadcast_to(y[None], (32, 8, 128)).reshape(256, 128)


def total(part):
    return pl.pallas_call(
        total_kernel,
        in_specs=[VM],
        out_specs=VM,
        out_shape=jax.ShapeDtypeStruct((256, 128), F32),
        compiler_params=pltpu.CompilerParams(vmem_limit_bytes=2 << 20),
        name="total",
    )(part)


def inverse_lower(aug, step):
    blocks = [aug[8 * b:8 * b + 8, :] for b in range(8)]
    sub = lax.broadcasted_iota(jnp.int32, (8, 128), 0)
    for k in range(0, 64, step):
        b0 = k // 8
        cols = [[jnp.broadcast_to(blocks[b][:, 64 + k + j:65 + k + j], (8, 128)) for b in range(b0, 8)]
                for j in range(step)]
        rows = [blocks[b0][k % 8 + j:k % 8 + j + 1, :] for j in range(step)]
        mult = []
        for j in range(step):
            r = k % 8 + j
            inv = 1.0 / cols[j][0][r:r + 1, :]
            l = [c * inv for c in cols[j]]
            l[0] = jnp.where(sub > r, l[0], 0.0)
            for j2 in range(j + 1, step):
                e = cols[j2][0][r:r + 1, :]
                cols[j2] = [c - x * e for c, x in zip(cols[j2], l)]
                rows[j2] = rows[j2] - l[0][r + j2 - j:r + j2 - j + 1, :] * rows[j]
            mult.append(l)
        for b in range(b0, 8):
            t = blocks[b]
            for j in range(step):
                t = t - mult[j][b - b0] * rows[j]
            blocks[b] = t
    lane = lax.broadcasted_iota(jnp.int32, (8, 128), 1)
    out = []
    for b in range(8):
        diag = jnp.sum(jnp.where(lane == sub + 64 + 8 * b, blocks[b], 0.0), axis=1, keepdims=True)
        out.append(blocks[b] * lax.rsqrt(diag))
    return jnp.concatenate(out, axis=0)[:, :64]


def orthonormal_t(yt, step):
    zero = jnp.zeros_like(yt)
    aug = nt(yt, jnp.concatenate([zero, yt], axis=0), HIGH)
    i = lax.broadcasted_iota(jnp.int32, aug.shape, 0)
    j = lax.broadcasted_iota(jnp.int32, aug.shape, 1)
    aug = jnp.where(i == j, 1.0, aug)
    return jnp.dot(inverse_lower(aug, step), yt, precision=HIGH, preferred_element_type=F32)


def core_kernel(y_ref, *refs):
    x_refs, (f_ref, o_ref) = refs[:-2], refs[-2:]
    s = len(x_refs)
    parts, m, w = x_refs[0].shape
    yt = jnp.concatenate([y_ref[c * 64:(c + 1) * 64, :] for c in range(4)], axis=1)
    ft = orthonormal_t(orthonormal_t(yt, 8), 8)
    f_ref[...] = ft
    low = ft.astype(BF16)
    i = lax.broadcasted_iota(jnp.int32, (64 * s, 64), 0)
    j = lax.broadcasted_iota(jnp.int32, (64 * s, 64), 1)
    wide = [jnp.dot((i == j * s + k).astype(BF16), low, preferred_element_type=F32).astype(BF16)
            for k in range(s)]
    step = 512
    for c in range(w // step):
        acc = None
        for k in range(s):
            x = x_refs[k][:, :, c * step:(c + 1) * step].reshape(parts * m, step)
            t = jnp.dot(wide[k], x, preferred_element_type=F32)
            acc = t if acc is None else acc + t
        o_ref[:, :, :, c * step:(c + 1) * step] = acc.astype(BF16).reshape(o_ref.shape[:3] + (step,))


def core_blocks(full, pieces):
    s = len(pieces)
    parts, _, w = pieces[0].shape
    return pl.pallas_call(
        core_kernel,
        in_specs=[VM] * (1 + s),
        out_specs=[VM, VM],
        out_shape=[jax.ShapeDtypeStruct((64, 512), F32),
                   jax.ShapeDtypeStruct((parts, 64 // parts, s, w), BF16)],
        compiler_params=pltpu.CompilerParams(vmem_limit_bytes=24 << 20),
        name="core",
    )(full, *pieces)


def merge_kernel(x_ref, o_ref, sem):
    parts, _, _, w = x_ref.shape
    copies = [pltpu.make_async_copy(x_ref.at[j], o_ref.at[:, :, pl.ds(j * w, w)], sem.at[j])
              for j in range(parts)]
    for c in copies:
        c.start()
    for c in copies:
        c.wait()


def merge_cells(core):
    parts, q, s, w = core.shape
    return pl.pallas_call(
        merge_kernel,
        in_specs=[VM],
        out_specs=ANY,
        out_shape=jax.ShapeDtypeStruct((q, s, parts * w), BF16),
        scratch_shapes=[pltpu.SemaphoreType.DMA((parts,))],
        compiler_params=pltpu.CompilerParams(vmem_limit_bytes=4 << 20),
        name="merge",
    )(core)


def body(fields, test_matrix):
    s, _, n = fields.shape
    parts = lax.axis_size("gx")
    axes = ("gx", "yz")
    scale = 1.0 / (s * n * lax.axis_size("yz"))
    order = ("x", "y", "x", "y")
    near = [None] * s
    for k in (0, 2):
        if k:
            fields, near[0][0] = lax.optimization_barrier((fields, near[0][0]))
        near[k], near[k + 1] = split_pair(fields[k:k + 2], parts)
    for k in (0, 2):
        far = [[near[k + i][0]] + [None] * 3 for i in range(2)]
        for d in (1, 3, 2):
            for i in range(2):
                far[i][d] = shift(near[k + i][d], order[k + i], d)
        near[k], near[k + 1] = far
    blocks = [None] * s
    for k in (0, 2):
        sent = regroup(near[k], near[k + 1])
        rest = [[None] * 3, [None] * 3]
        for d in (1, 3, 2):
            for i in range(2):
                rest[i][d - 1] = shift(sent[i][d - 1], order[1 - i], d)
        for i in range(2):
            blocks[k + i] = list(near[k + i]) + rest[i]
    pieces = [None] * s
    part = None
    for k in range(s):
        pieces[k], part = add_gram(order[k], blocks[k], part, test_matrix.T if k == s - 1 else None, scale)
    part = lax.all_to_all(part.reshape(128, 2, 128), axes, split_axis=0, concat_axis=0, tiled=True)
    part = total(part.reshape(256, 128))
    full = lax.all_to_all(part.reshape(128, 2, 128), axes, split_axis=0, concat_axis=0, tiled=True)
    ft, core = core_blocks(full.reshape(256, 128), pieces)
    core = lax.all_to_all(core, "gx", split_axis=0, concat_axis=0, tiled=True)
    return (ft.T, merge_cells(core))


def solution(mesh):
    in_specs = (P(None, "gx", "yz"), P())
    out_specs = (P(), P("gx", None, "yz"))
    return jax.shard_map(body, mesh=mesh, in_specs=in_specs, out_specs=out_specs, check_vma=False)
```

```python
import jax
import jax.numpy as jnp
from jax import lax
from jax.sharding import PartitionSpec as P
from jax.experimental import pallas as pl
from jax.experimental.pallas import tpu as pltpu

F32 = jnp.float32
CUTS = {0: 1, 2: 2}
BF16 = jnp.bfloat16
VM = pl.BlockSpec(memory_space=pltpu.VMEM)
ANY = pl.BlockSpec(memory_space=pl.ANY)


def nt(a, b, precision=None):
    return lax.dot_general(a, b, (((1,), (1,)), ((), ())), precision=precision,
                           preferred_element_type=F32)


def nn(a, b):
    return jnp.dot(a, b, preferred_element_type=F32)


def cut3(v):
    terms = []
    for _ in range(3):
        t = v.astype(BF16)
        terms.append(t)
        v = v - t.astype(F32)
    return terms


def place():
    g = lax.axis_index("gx")
    return lax.rem(g, 4), lax.div(g, 4)


def member(x, y):
    return lax.rem(y + 4, 4) * 4 + lax.rem(x + 4, 4)


def split_kernel(x_ref, *outs):
    w = outs[0].shape[-1]
    x, y = place()
    for k in range(2):
        for d in range(4):
            for q in range(4):
                j = member(x + q, y + d) if k else member(x + d, y + q)
                outs[4 * k + d][q] = x_ref[k, :, pl.ds(pl.multiple_of(j * w, w), w)]


def split_pair(pair, parts):
    _, m, n = pair.shape
    out = jax.ShapeDtypeStruct((4, m, n // parts), pair.dtype)
    outs = pl.pallas_call(
        split_kernel,
        in_specs=[VM],
        out_specs=[VM] * 8,
        out_shape=[out] * 8,
        compiler_params=pltpu.CompilerParams(vmem_limit_bytes=10 << 20),
        cost_estimate=pl.CostEstimate(flops=0, transcendentals=0, bytes_accessed=8 * m * n),
        name="split",
    )(pair)
    return list(outs[:4]), list(outs[4:])


def fetch_split_kernel(first, x_ref, *refs):
    outs, (buf, sem) = refs[:8], refs[8:]
    loads = [pltpu.make_async_copy(x_ref.at[first + k], buf.at[k], sem.at[k]) for k in range(2)]
    for c in loads:
        c.start()
    for c in loads:
        c.wait()
    split_kernel(buf, *outs)


def fetch_split_pair(fields, first, parts):
    _, m, n = fields.shape
    out = jax.ShapeDtypeStruct((4, m, n // parts), fields.dtype)
    outs = pl.pallas_call(
        lambda *r: fetch_split_kernel(first, *r),
        in_specs=[ANY],
        out_specs=[VM] * 8,
        out_shape=[out] * 8,
        scratch_shapes=[pltpu.VMEM((2, m, n), fields.dtype), pltpu.SemaphoreType.DMA((2,))],
        compiler_params=pltpu.CompilerParams(vmem_limit_bytes=50 << 20),
        cost_estimate=pl.CostEstimate(flops=0, transcendentals=0, bytes_accessed=8 * m * n),
        name="fetch_split",
    )(fields)
    return list(outs[:4]), list(outs[4:])


def shift(v, along, d):
    step = 1 if along == "x" else 4
    pairs = []
    for g in range(16):
        c = (g // step) % 4
        pairs.append((g, g + ((c + d) % 4 - c) * step))
    return lax.ppermute(v, "gx", pairs)


def regroup_kernel(cuts, *refs):
    outs = list(refs[8:])
    for k in range(2):
        got = refs[4 * k:4 * k + 4]
        w = got[0].shape[-1] // cuts
        for h in range(cuts):
            for q in range(1, 4):
                out = outs.pop(0)
                for d in range(4):
                    out[d] = got[d][q, :, h * w:(h + 1) * w]


def regroup(one, two, cuts):
    n, m, w = one[0].shape
    out = jax.ShapeDtypeStruct((n, m, w // cuts), one[0].dtype)
    outs = pl.pallas_call(
        lambda *r: regroup_kernel(cuts, *r),
        in_specs=[VM] * 8,
        out_specs=[VM] * (6 * cuts),
        out_shape=[out] * (6 * cuts),
        compiler_params=pltpu.CompilerParams(vmem_limit_bytes=6 << 20),
        cost_estimate=pl.CostEstimate(flops=0, transcendentals=0, bytes_accessed=4 * one[0].size),
        name="regroup",
    )(*one, *two)
    return [[outs[3 * (cuts * k + h):3 * (cuts * k + h) + 3] for k in range(2)] for h in range(cuts)]


def gram_kernel(cut, scale, *refs):
    blocks, rest = (refs[:7], refs[7:14]), list(refs[14:])
    acc = rest.pop(0) if len(rest) > 3 else None
    t_ref = rest.pop(0) if len(rest) > 3 else None
    p_refs, o_ref = rest[:2], rest[2]
    parts, m, w = p_refs[0].shape
    x, y = place()
    h = parts * m // 2
    gram = None if acc is None else [acc[k] for k in range(3)]
    for k in range(2):
        for d1 in range(4):
            for d2 in range(4):
                g = member(x - d2, y - d1) if k else member(x - d1, y - d2)
                if d2 == 0:
                    p_refs[k][g] = blocks[k][d1][0, :, cut * w:(cut + 1) * w]
                else:
                    p_refs[k][g] = blocks[k][3 + d2][d1]
    for k in range(2):
        top = p_refs[k][:parts // 2].reshape(h, w)
        low = p_refs[k][parts // 2:].reshape(h, w)
        more = [nt(p, q) for p, q in ((top, top), (top, low), (low, low))]
        gram = more if gram is None else [p + q for p, q in zip(gram, more)]
    if t_ref is None:
        for k in range(3):
            o_ref[k] = gram[k]
        return
    terms = cut3(t_ref[...])
    one, two = (jnp.concatenate([t[:, k * h:(k + 1) * h] for t in terms], axis=0) for k in range(2))
    (top, mid, low) = (cut3(g) for g in gram)

    def times(t, g, dot):
        r = dot(t, g[0]), dot(t[:128], g[1]), dot(t[:64], g[2])
        return (r[0][128:] + r[1][64:] + r[2]) + (r[0][64:128] + r[1][:64]) + r[0][:64]

    left = times(one, top, nn) + times(two, mid, nt)
    right = times(one, mid, nn) + times(two, low, nn)
    sk = jnp.concatenate([left, right], axis=1) * scale
    for c in range(4):
        o_ref[c * 64:(c + 1) * 64, :] = sk[:, c * 128:(c + 1) * 128]


def add_gram(blocks, cut, acc=None, test_t=None, scale=1.0):
    _, m, w = blocks[-1].shape
    args = list(blocks) + [v for v in (acc, test_t) if v is not None]
    shape = (3, 256, 256) if test_t is None else (256, 128)
    fibres = jax.ShapeDtypeStruct((16, m, w), BF16)
    return pl.pallas_call(
        lambda *r: gram_kernel(cut, scale, *r),
        in_specs=[VM] * len(args),
        out_specs=[VM] * 3,
        out_shape=[fibres, fibres, jax.ShapeDtypeStruct(shape, F32)],
        compiler_params=pltpu.CompilerParams(vmem_limit_bytes=16 << 20),
        cost_estimate=pl.CostEstimate(flops=6 * 2 * 256 * 256 * w, transcendentals=0,
                                      bytes_accessed=32 * m * w * 4),
        name="gram",
    )(*args)


def total_kernel(x_ref, o_ref):
    y = jnp.sum(x_ref[...].reshape(-1, 8, 128), axis=0)
    y = y + pltpu.roll(y, 4, 0)
    y = y + pltpu.roll(y, 2, 0)
    o_ref[...] = jnp.broadcast_to(y[None], (32, 8, 128)).reshape(256, 128)


def total(part):
    return pl.pallas_call(
        total_kernel,
        in_specs=[VM],
        out_specs=VM,
        out_shape=jax.ShapeDtypeStruct((256, 128), F32),
        compiler_params=pltpu.CompilerParams(vmem_limit_bytes=2 << 20),
        name="total",
    )(part)


def inverse_lower(aug, step):
    blocks = [aug[8 * b:8 * b + 8, :] for b in range(8)]
    sub = lax.broadcasted_iota(jnp.int32, (8, 128), 0)
    for k in range(0, 64, step):
        b0 = k // 8
        cols = [[jnp.broadcast_to(blocks[b][:, 64 + k + j:65 + k + j], (8, 128)) for b in range(b0, 8)]
                for j in range(step)]
        rows = [blocks[b0][k % 8 + j:k % 8 + j + 1, :] for j in range(step)]
        mult = []
        for j in range(step):
            r = k % 8 + j
            inv = 1.0 / cols[j][0][r:r + 1, :]
            l = [c * inv for c in cols[j]]
            l[0] = jnp.where(sub > r, l[0], 0.0)
            for j2 in range(j + 1, step):
                e = cols[j2][0][r:r + 1, :]
                cols[j2] = [c - x * e for c, x in zip(cols[j2], l)]
                rows[j2] = rows[j2] - l[0][r + j2 - j:r + j2 - j + 1, :] * rows[j]
            mult.append(l)
        for b in range(b0, 8):
            t = blocks[b]
            for j in range(step):
                t = t - mult[j][b - b0] * rows[j]
            blocks[b] = t
    lane = lax.broadcasted_iota(jnp.int32, (8, 128), 1)
    out = []
    for b in range(8):
        diag = jnp.sum(jnp.where(lane == sub + 64 + 8 * b, blocks[b], 0.0), axis=1, keepdims=True)
        out.append(blocks[b] * lax.rsqrt(diag))
    return jnp.concatenate(out, axis=0)[:, :64]


def orthonormal_t(yt, step):
    n = yt.shape[0]
    terms = cut3(yt)
    tall = jnp.concatenate(terms, axis=0)
    nine = nt(tall, jnp.concatenate([tall, jnp.zeros_like(terms[0])], axis=0))
    rows = (nine[2 * n:] + nine[n:2 * n]) + nine[:n]
    near, far = rows[:, :2 * n], rows[:, 2 * n:]
    aug = (far + pltpu.roll(far, n, 1)) + (near + pltpu.roll(near, n, 1))
    i = lax.broadcasted_iota(jnp.int32, aug.shape, 0)
    j = lax.broadcasted_iota(jnp.int32, aug.shape, 1)
    aug = jnp.where(j < n, (i == j).astype(F32), aug)
    inv = cut3(inverse_lower(aug, step))
    tall = jnp.concatenate(inv, axis=0)
    r = nn(tall, terms[0]), nn(tall[:2 * n], terms[1]), nn(tall[:n], terms[2])
    return (r[0][2 * n:] + r[1][n:] + r[2]) + (r[0][n:2 * n] + r[1][:n]) + r[0][:n]


def cells_of(x_refs, k, at):
    if k < 2:
        return x_refs[k], at
    w = x_refs[2].shape[-1]
    return x_refs[2 + k - 2 + 2 * (at // w)], at % w


def core_kernel(y_ref, *refs):
    x_refs, (f_ref, o_ref) = refs[:-2], refs[-2:]
    _, _, s, w = o_ref.shape
    parts, m, _ = x_refs[0].shape
    yt = jnp.concatenate([y_ref[c * 64:(c + 1) * 64, :] for c in range(4)], axis=1)
    ft = orthonormal_t(orthonormal_t(yt, 8), 8)
    f_ref[...] = ft
    low = ft.astype(BF16)
    i = lax.broadcasted_iota(jnp.int32, (64 * s, 64), 0)
    j = lax.broadcasted_iota(jnp.int32, (64 * s, 64), 1)
    wide = [jnp.dot((i == j * s + k).astype(BF16), low, preferred_element_type=F32).astype(BF16)
            for k in range(s)]
    step = 512
    for c in range(w // step):
        acc = None
        for k in range(s):
            x_ref, at = cells_of(x_refs, k, c * step)
            x = x_ref[:, :, at:at + step].reshape(parts * m, step)
            t = jnp.dot(wide[k], x, preferred_element_type=F32)
            acc = t if acc is None else acc + t
        o_ref[:, :, :, c * step:(c + 1) * step] = acc.astype(BF16).reshape(o_ref.shape[:3] + (step,))


def core_blocks(full, pieces, s):
    parts, _, w = pieces[0].shape
    return pl.pallas_call(
        core_kernel,
        in_specs=[VM] * (1 + len(pieces)),
        out_specs=[VM, VM],
        out_shape=[jax.ShapeDtypeStruct((64, 512), F32),
                   jax.ShapeDtypeStruct((parts, 64 // parts, s, w), BF16)],
        compiler_params=pltpu.CompilerParams(vmem_limit_bytes=24 << 20),
        name="core",
    )(full, *pieces)


def merge_kernel(x_ref, o_ref, sem):
    parts, _, _, w = x_ref.shape
    copies = [pltpu.make_async_copy(x_ref.at[j], o_ref.at[:, :, pl.ds(j * w, w)], sem.at[j])
              for j in range(parts)]
    for c in copies:
        c.start()
    for c in copies:
        c.wait()


def merge_cells(core):
    parts, q, s, w = core.shape
    return pl.pallas_call(
        merge_kernel,
        in_specs=[VM],
        out_specs=ANY,
        out_shape=jax.ShapeDtypeStruct((q, s, parts * w), BF16),
        scratch_shapes=[pltpu.SemaphoreType.DMA((parts,))],
        compiler_params=pltpu.CompilerParams(vmem_limit_bytes=4 << 20),
        name="merge",
    )(core)


def body(fields, test_matrix):
    s, _, n = fields.shape
    parts = lax.axis_size("gx")
    axes = ("gx", "yz")
    scale = 1.0 / (s * n * lax.axis_size("yz"))
    order = ("x", "y", "x", "y")
    near = [None] * s
    near[0], near[1] = split_pair(fields[:2], parts)
    near[2], near[3] = fetch_split_pair(fields, 2, parts)
    for k in (0, 2):
        far = [[near[k + i][0]] + [None] * 3 for i in range(2)]
        for d in (1, 3, 2):
            for i in range(2):
                far[i][d] = shift(near[k + i][d], order[k + i], d)
        near[k], near[k + 1] = far
    blocks = {}
    for k in (0, 2):
        for h, sent in enumerate(regroup(near[k], near[k + 1], CUTS[k])):
            rest = [[None] * 3, [None] * 3]
            for d in (1, 3, 2):
                for i in range(2):
                    rest[i][d - 1] = shift(sent[i][d - 1], order[1 - i], d)
            blocks[k, h] = near[k] + rest[0] + near[k + 1] + rest[1]
    pieces, part = [], None
    for (k, h), block in blocks.items():
        last = (k, h) == (2, CUTS[2] - 1)
        *more, part = add_gram(block, h, part, test_matrix.T if last else None, scale)
        pieces += more
    part = lax.all_to_all(part.reshape(128, 2, 128), axes, split_axis=0, concat_axis=0, tiled=True)
    part = total(part.reshape(256, 128))
    full = lax.all_to_all(part.reshape(128, 2, 128), axes, split_axis=0, concat_axis=0, tiled=True)
    ft, core = core_blocks(full.reshape(256, 128), pieces, s)
    core = lax.all_to_all(core, "gx", split_axis=0, concat_axis=0, tiled=True)
    return (ft.T, merge_cells(core))


def solution(mesh):
    in_specs = (P(None, "gx", "yz"), P())
    out_specs = (P(), P("gx", None, "yz"))
    return jax.shard_map(body, mesh=mesh, in_specs=in_specs, out_specs=out_specs, check_vma=False)
```

```python
import jax
import jax.numpy as jnp
from jax import lax
from jax.sharding import PartitionSpec as P
from jax.experimental import pallas as pl
from jax.experimental.pallas import tpu as pltpu

F32 = jnp.float32
CUTS = {0: (0, 4), 2: (0, 3, 4)}
BF16 = jnp.bfloat16
VM = pl.BlockSpec(memory_space=pltpu.VMEM)
ANY = pl.BlockSpec(memory_space=pl.ANY)


def nt(a, b, precision=None):
    return lax.dot_general(a, b, (((1,), (1,)), ((), ())), precision=precision,
                           preferred_element_type=F32)


def nn(a, b):
    return jnp.dot(a, b, preferred_element_type=F32)


def cut3(v):
    terms = []
    for _ in range(3):
        t = v.astype(BF16)
        terms.append(t)
        v = v - t.astype(F32)
    return terms


def place():
    g = lax.axis_index("gx")
    return lax.rem(g, 4), lax.div(g, 4)


def member(x, y):
    return lax.rem(y + 4, 4) * 4 + lax.rem(x + 4, 4)


def split_kernel(x_ref, *outs):
    w = outs[0].shape[-1]
    x, y = place()
    for k in range(2):
        for d in range(4):
            for q in range(4):
                j = member(x + q, y + d) if k else member(x + d, y + q)
                outs[4 * k + d][q] = x_ref[k, :, pl.ds(pl.multiple_of(j * w, w), w)]


def split_pair(pair, parts):
    _, m, n = pair.shape
    out = jax.ShapeDtypeStruct((4, m, n // parts), pair.dtype)
    outs = pl.pallas_call(
        split_kernel,
        in_specs=[VM],
        out_specs=[VM] * 8,
        out_shape=[out] * 8,
        compiler_params=pltpu.CompilerParams(vmem_limit_bytes=10 << 20),
        cost_estimate=pl.CostEstimate(flops=0, transcendentals=0, bytes_accessed=8 * m * n),
        name="split",
    )(pair)
    return list(outs[:4]), list(outs[4:])


def fetch_split_kernel(first, x_ref, *refs):
    outs, (buf, sem) = refs[:8], refs[8:]
    loads = [pltpu.make_async_copy(x_ref.at[first + k], buf.at[k], sem.at[k]) for k in range(2)]
    for c in loads:
        c.start()
    for c in loads:
        c.wait()
    split_kernel(buf, *outs)


def fetch_split_pair(fields, first, parts):
    _, m, n = fields.shape
    out = jax.ShapeDtypeStruct((4, m, n // parts), fields.dtype)
    outs = pl.pallas_call(
        lambda *r: fetch_split_kernel(first, *r),
        in_specs=[ANY],
        out_specs=[VM] * 8,
        out_shape=[out] * 8,
        scratch_shapes=[pltpu.VMEM((2, m, n), fields.dtype), pltpu.SemaphoreType.DMA((2,))],
        compiler_params=pltpu.CompilerParams(vmem_limit_bytes=50 << 20),
        cost_estimate=pl.CostEstimate(flops=0, transcendentals=0, bytes_accessed=8 * m * n),
        name="fetch_split",
    )(fields)
    return list(outs[:4]), list(outs[4:])


def shift(v, along, d):
    step = 1 if along == "x" else 4
    pairs = []
    for g in range(16):
        c = (g // step) % 4
        pairs.append((g, g + ((c + d) % 4 - c) * step))
    return lax.ppermute(v, "gx", pairs)


def pieces_of(cuts, w):
    return [(p * w // 4, q * w // 4) for p, q in zip(cuts, cuts[1:])]


def regroup_kernel(cuts, *refs):
    outs = list(refs[8:])
    for k in range(2):
        got = refs[4 * k:4 * k + 4]
        for lo, hi in pieces_of(cuts, got[0].shape[-1]):
            for q in range(1, 4):
                out = outs.pop(0)
                for d in range(4):
                    out[d] = got[d][q, :, lo:hi]


def regroup(one, two, cuts):
    n, m, w = one[0].shape
    count = len(cuts) - 1
    shapes = [jax.ShapeDtypeStruct((n, m, hi - lo), one[0].dtype)
              for lo, hi in pieces_of(cuts, w) for _ in range(3)]
    outs = pl.pallas_call(
        lambda *r: regroup_kernel(cuts, *r),
        in_specs=[VM] * 8,
        out_specs=[VM] * (6 * count),
        out_shape=shapes * 2,
        compiler_params=pltpu.CompilerParams(vmem_limit_bytes=6 << 20),
        cost_estimate=pl.CostEstimate(flops=0, transcendentals=0, bytes_accessed=4 * one[0].size),
        name="regroup",
    )(*one, *two)
    return [[outs[3 * (count * k + h):3 * (count * k + h) + 3] for k in range(2)] for h in range(count)]


def gram_kernel(cut, scale, *refs):
    blocks, rest = (refs[:7], refs[7:14]), list(refs[14:])
    acc = rest.pop(0) if len(rest) > 3 else None
    t_ref = rest.pop(0) if len(rest) > 3 else None
    p_refs, o_ref = rest[:2], rest[2]
    parts, m, w = p_refs[0].shape
    x, y = place()
    h = parts * m // 2
    gram = None if acc is None else [acc[k] for k in range(3)]
    for k in range(2):
        for d1 in range(4):
            for d2 in range(4):
                g = member(x - d2, y - d1) if k else member(x - d1, y - d2)
                if d2 == 0:
                    p_refs[k][g] = blocks[k][d1][0, :, cut:cut + w]
                else:
                    p_refs[k][g] = blocks[k][3 + d2][d1]
    for k in range(2):
        top = p_refs[k][:parts // 2].reshape(h, w)
        low = p_refs[k][parts // 2:].reshape(h, w)
        more = [nt(p, q) for p, q in ((top, top), (top, low), (low, low))]
        gram = more if gram is None else [p + q for p, q in zip(gram, more)]
    if t_ref is None:
        for k in range(3):
            o_ref[k] = gram[k]
        return
    terms = cut3(t_ref[...])
    one, two = (jnp.concatenate([t[:, k * h:(k + 1) * h] for t in terms], axis=0) for k in range(2))
    (top, mid, low) = (cut3(g) for g in gram)

    def times(t, g, dot):
        r = dot(t, g[0]), dot(t[:128], g[1]), dot(t[:64], g[2])
        return (r[0][128:] + r[1][64:] + r[2]) + (r[0][64:128] + r[1][:64]) + r[0][:64]

    left = times(one, top, nn) + times(two, mid, nt)
    right = times(one, mid, nn) + times(two, low, nn)
    sk = jnp.concatenate([left, right], axis=1) * scale
    for c in range(4):
        o_ref[c * 64:(c + 1) * 64, :] = sk[:, c * 128:(c + 1) * 128]


def add_gram(blocks, cut, acc=None, test_t=None, scale=1.0):
    _, m, w = blocks[-1].shape
    args = list(blocks) + [v for v in (acc, test_t) if v is not None]
    shape = (3, 256, 256) if test_t is None else (256, 128)
    fibres = jax.ShapeDtypeStruct((16, m, w), BF16)
    return pl.pallas_call(
        lambda *r: gram_kernel(cut, scale, *r),
        in_specs=[VM] * len(args),
        out_specs=[VM] * 3,
        out_shape=[fibres, fibres, jax.ShapeDtypeStruct(shape, F32)],
        compiler_params=pltpu.CompilerParams(vmem_limit_bytes=16 << 20),
        cost_estimate=pl.CostEstimate(flops=6 * 2 * 256 * 256 * w, transcendentals=0,
                                      bytes_accessed=32 * m * w * 4),
        name="gram",
    )(*args)


def total_kernel(x_ref, o_ref):
    y = jnp.sum(x_ref[...].reshape(-1, 8, 128), axis=0)
    y = y + pltpu.roll(y, 4, 0)
    y = y + pltpu.roll(y, 2, 0)
    o_ref[...] = jnp.broadcast_to(y[None], (32, 8, 128)).reshape(256, 128)


def total(part):
    return pl.pallas_call(
        total_kernel,
        in_specs=[VM],
        out_specs=VM,
        out_shape=jax.ShapeDtypeStruct((256, 128), F32),
        compiler_params=pltpu.CompilerParams(vmem_limit_bytes=2 << 20),
        name="total",
    )(part)


def inverse_lower(aug, step):
    blocks = [aug[8 * b:8 * b + 8, :] for b in range(8)]
    sub = lax.broadcasted_iota(jnp.int32, (8, 128), 0)
    for k in range(0, 64, step):
        b0 = k // 8
        cols = [[jnp.broadcast_to(blocks[b][:, 64 + k + j:65 + k + j], (8, 128)) for b in range(b0, 8)]
                for j in range(step)]
        rows = [blocks[b0][k % 8 + j:k % 8 + j + 1, :] for j in range(step)]
        mult = []
        for j in range(step):
            r = k % 8 + j
            inv = 1.0 / cols[j][0][r:r + 1, :]
            l = [c * inv for c in cols[j]]
            l[0] = jnp.where(sub > r, l[0], 0.0)
            for j2 in range(j + 1, step):
                e = cols[j2][0][r:r + 1, :]
                cols[j2] = [c - x * e for c, x in zip(cols[j2], l)]
                rows[j2] = rows[j2] - l[0][r + j2 - j:r + j2 - j + 1, :] * rows[j]
            mult.append(l)
        for b in range(b0, 8):
            t = blocks[b]
            for j in range(step):
                t = t - mult[j][b - b0] * rows[j]
            blocks[b] = t
    lane = lax.broadcasted_iota(jnp.int32, (8, 128), 1)
    out = []
    for b in range(8):
        diag = jnp.sum(jnp.where(lane == sub + 64 + 8 * b, blocks[b], 0.0), axis=1, keepdims=True)
        out.append(blocks[b] * lax.rsqrt(diag))
    return jnp.concatenate(out, axis=0)[:, :64]


def orthonormal_t(yt, step):
    n = yt.shape[0]
    terms = cut3(yt)
    tall = jnp.concatenate(terms, axis=0)
    nine = nt(tall, jnp.concatenate([tall, jnp.zeros_like(terms[0])], axis=0))
    rows = (nine[2 * n:] + nine[n:2 * n]) + nine[:n]
    near, far = rows[:, :2 * n], rows[:, 2 * n:]
    aug = (far + pltpu.roll(far, n, 1)) + (near + pltpu.roll(near, n, 1))
    i = lax.broadcasted_iota(jnp.int32, aug.shape, 0)
    j = lax.broadcasted_iota(jnp.int32, aug.shape, 1)
    aug = jnp.where(j < n, (i == j).astype(F32), aug)
    inv = cut3(inverse_lower(aug, step))
    tall = jnp.concatenate(inv, axis=0)
    r = nn(tall, terms[0]), nn(tall[:2 * n], terms[1]), nn(tall[:n], terms[2])
    return (r[0][2 * n:] + r[1][n:] + r[2]) + (r[0][n:2 * n] + r[1][:n]) + r[0][:n]


def cells_of(x_refs, k, at):
    if k < 2:
        return x_refs[k], at
    w = x_refs[2].shape[-1]
    return (x_refs[k], at) if at < w else (x_refs[k + 2], at - w)


def core_kernel(y_ref, *refs):
    x_refs, (f_ref, o_ref) = refs[:-2], refs[-2:]
    _, _, s, w = o_ref.shape
    parts, m, _ = x_refs[0].shape
    yt = jnp.concatenate([y_ref[c * 64:(c + 1) * 64, :] for c in range(4)], axis=1)
    ft = orthonormal_t(orthonormal_t(yt, 8), 8)
    f_ref[...] = ft
    low = ft.astype(BF16)
    i = lax.broadcasted_iota(jnp.int32, (64 * s, 64), 0)
    j = lax.broadcasted_iota(jnp.int32, (64 * s, 64), 1)
    wide = [jnp.dot((i == j * s + k).astype(BF16), low, preferred_element_type=F32).astype(BF16)
            for k in range(s)]
    step = 512
    for c in range(w // step):
        acc = None
        for k in range(s):
            x_ref, at = cells_of(x_refs, k, c * step)
            x = x_ref[:, :, at:at + step].reshape(parts * m, step)
            t = jnp.dot(wide[k], x, preferred_element_type=F32)
            acc = t if acc is None else acc + t
        o_ref[:, :, :, c * step:(c + 1) * step] = acc.astype(BF16).reshape(o_ref.shape[:3] + (step,))


def core_blocks(full, pieces, s):
    parts, _, w = pieces[0].shape
    return pl.pallas_call(
        core_kernel,
        in_specs=[VM] * (1 + len(pieces)),
        out_specs=[VM, VM],
        out_shape=[jax.ShapeDtypeStruct((64, 512), F32),
                   jax.ShapeDtypeStruct((parts, 64 // parts, s, w), BF16)],
        compiler_params=pltpu.CompilerParams(vmem_limit_bytes=24 << 20),
        name="core",
    )(full, *pieces)


def merge_kernel(x_ref, o_ref, sem):
    parts, _, _, w = x_ref.shape
    copies = [pltpu.make_async_copy(x_ref.at[j], o_ref.at[:, :, pl.ds(j * w, w)], sem.at[j])
              for j in range(parts)]
    for c in copies:
        c.start()
    for c in copies:
        c.wait()


def merge_cells(core):
    parts, q, s, w = core.shape
    return pl.pallas_call(
        merge_kernel,
        in_specs=[VM],
        out_specs=ANY,
        out_shape=jax.ShapeDtypeStruct((q, s, parts * w), BF16),
        scratch_shapes=[pltpu.SemaphoreType.DMA((parts,))],
        compiler_params=pltpu.CompilerParams(vmem_limit_bytes=4 << 20),
        name="merge",
    )(core)


def body(fields, test_matrix):
    s, _, n = fields.shape
    parts = lax.axis_size("gx")
    w = n // parts
    axes = ("gx", "yz")
    scale = 1.0 / (s * n * lax.axis_size("yz"))
    order = ("x", "y", "x", "y")
    near = [None] * s
    near[0], near[1] = split_pair(fields[:2], parts)
    near[2], near[3] = fetch_split_pair(fields, 2, parts)
    for k in (0, 2):
        far = [[near[k + i][0]] + [None] * 3 for i in range(2)]
        for d in (1, 3, 2):
            for i in range(2):
                far[i][d] = shift(near[k + i][d], order[k + i], d)
        near[k], near[k + 1] = far
    blocks = {}
    for k in (0, 2):
        for h, sent in enumerate(regroup(near[k], near[k + 1], CUTS[k])):
            rest = [[None] * 3, [None] * 3]
            for d in (1, 3, 2):
                for i in range(2):
                    rest[i][d - 1] = shift(sent[i][d - 1], order[1 - i], d)
            blocks[k, h] = near[k] + rest[0] + near[k + 1] + rest[1]
    pieces, part = [], None
    for (k, h), block in blocks.items():
        last = (k, h) == (2, len(CUTS[2]) - 2)
        *more, part = add_gram(block, pieces_of(CUTS[k], w)[h][0], part, test_matrix.T if last else None, scale)
        pieces += more
    part = lax.all_to_all(part.reshape(128, 2, 128), axes, split_axis=0, concat_axis=0, tiled=True)
    part = total(part.reshape(256, 128))
    full = lax.all_to_all(part.reshape(128, 2, 128), axes, split_axis=0, concat_axis=0, tiled=True)
    ft, core = core_blocks(full.reshape(256, 128), pieces, s)
    core = lax.all_to_all(core, "gx", split_axis=0, concat_axis=0, tiled=True)
    return (ft.T, merge_cells(core))


def solution(mesh):
    in_specs = (P(None, "gx", "yz"), P())
    out_specs = (P(), P("gx", None, "yz"))
    return jax.shard_map(body, mesh=mesh, in_specs=in_specs, out_specs=out_specs, check_vma=False)
```

```python
import jax
import jax.numpy as jnp
from jax import lax
from jax.sharding import PartitionSpec as P
from jax.experimental import pallas as pl
from jax.experimental.pallas import tpu as pltpu

F32 = jnp.float32
CUTS = {0: (0, 4), 2: (0, 3, 4)}
BF16 = jnp.bfloat16
VM = pl.BlockSpec(memory_space=pltpu.VMEM)
ANY = pl.BlockSpec(memory_space=pl.ANY)


def nt(a, b, precision=None):
    return lax.dot_general(a, b, (((1,), (1,)), ((), ())), precision=precision,
                           preferred_element_type=F32)


def nn(a, b):
    return jnp.dot(a, b, preferred_element_type=F32)


def cut3(v):
    terms = []
    for _ in range(3):
        t = v.astype(BF16)
        terms.append(t)
        v = v - t.astype(F32)
    return terms


def place():
    g = lax.axis_index("gx")
    return lax.rem(g, 4), lax.div(g, 4)


def member(x, y):
    return lax.rem(y + 4, 4) * 4 + lax.rem(x + 4, 4)


def split_kernel(x_ref, *outs):
    w = outs[0].shape[-1]
    x, y = place()
    for k in range(2):
        for d in range(4):
            for q in range(4):
                j = member(x + q, y + d) if k else member(x + d, y + q)
                outs[4 * k + d][q] = x_ref[k, :, pl.ds(pl.multiple_of(j * w, w), w)]


def split_pair(pair, parts):
    _, m, n = pair.shape
    out = jax.ShapeDtypeStruct((4, m, n // parts), pair.dtype)
    outs = pl.pallas_call(
        split_kernel,
        in_specs=[VM],
        out_specs=[VM] * 8,
        out_shape=[out] * 8,
        compiler_params=pltpu.CompilerParams(vmem_limit_bytes=10 << 20),
        cost_estimate=pl.CostEstimate(flops=0, transcendentals=0, bytes_accessed=8 * m * n),
        name="split",
    )(pair)
    return list(outs[:4]), list(outs[4:])


def fetch_split_kernel(first, x_ref, *refs):
    outs, (buf, sem) = refs[:8], refs[8:]
    loads = [pltpu.make_async_copy(x_ref.at[first + k], buf.at[k], sem.at[k]) for k in range(2)]
    for c in loads:
        c.start()
    for c in loads:
        c.wait()
    split_kernel(buf, *outs)


def fetch_split_pair(fields, first, parts):
    _, m, n = fields.shape
    out = jax.ShapeDtypeStruct((4, m, n // parts), fields.dtype)
    outs = pl.pallas_call(
        lambda *r: fetch_split_kernel(first, *r),
        in_specs=[ANY],
        out_specs=[VM] * 8,
        out_shape=[out] * 8,
        scratch_shapes=[pltpu.VMEM((2, m, n), fields.dtype), pltpu.SemaphoreType.DMA((2,))],
        compiler_params=pltpu.CompilerParams(vmem_limit_bytes=50 << 20),
        cost_estimate=pl.CostEstimate(flops=0, transcendentals=0, bytes_accessed=8 * m * n),
        name="fetch_split",
    )(fields)
    return list(outs[:4]), list(outs[4:])


def shift(v, along, d):
    step = 1 if along == "x" else 4
    pairs = []
    for g in range(16):
        c = (g // step) % 4
        pairs.append((g, g + ((c + d) % 4 - c) * step))
    return lax.ppermute(v, "gx", pairs)


def pieces_of(cuts, w):
    return [(p * w // 4, q * w // 4) for p, q in zip(cuts, cuts[1:])]


def regroup_kernel(cuts, *refs):
    outs = list(refs[8:])
    for k in range(2):
        got = refs[4 * k:4 * k + 4]
        for lo, hi in pieces_of(cuts, got[0].shape[-1]):
            for q in range(1, 4):
                out = outs.pop(0)
                for d in range(4):
                    out[d] = got[d][q, :, lo:hi]


def regroup(one, two, cuts):
    n, m, w = one[0].shape
    count = len(cuts) - 1
    shapes = [jax.ShapeDtypeStruct((n, m, hi - lo), one[0].dtype)
              for lo, hi in pieces_of(cuts, w) for _ in range(3)]
    outs = pl.pallas_call(
        lambda *r: regroup_kernel(cuts, *r),
        in_specs=[VM] * 8,
        out_specs=[VM] * (6 * count),
        out_shape=shapes * 2,
        compiler_params=pltpu.CompilerParams(vmem_limit_bytes=6 << 20),
        cost_estimate=pl.CostEstimate(flops=0, transcendentals=0, bytes_accessed=4 * one[0].size),
        name="regroup",
    )(*one, *two)
    return [[outs[3 * (count * k + h):3 * (count * k + h) + 3] for k in range(2)] for h in range(count)]


def gram_kernel(cut, scale, *refs):
    blocks, rest = (refs[:7], refs[7:14]), list(refs[14:])
    acc = rest.pop(0) if len(rest) > 3 else None
    t_ref = rest.pop(0) if len(rest) > 3 else None
    p_refs, o_ref = rest[:2], rest[2]
    parts, m, w = p_refs[0].shape
    x, y = place()
    h = parts * m // 2
    gram = None if acc is None else [acc[k] for k in range(3)]
    for k in range(2):
        for d1 in range(4):
            for d2 in range(4):
                g = member(x - d2, y - d1) if k else member(x - d1, y - d2)
                if d2 == 0:
                    p_refs[k][g] = blocks[k][d1][0, :, cut:cut + w]
                else:
                    p_refs[k][g] = blocks[k][3 + d2][d1]
    for k in range(2):
        top = p_refs[k][:parts // 2].reshape(h, w)
        low = p_refs[k][parts // 2:].reshape(h, w)
        more = [nt(p, q) for p, q in ((top, top), (top, low), (low, low))]
        gram = more if gram is None else [p + q for p, q in zip(gram, more)]
    if t_ref is None:
        for k in range(3):
            o_ref[k] = gram[k]
        return
    terms = cut3(t_ref[...])
    one, two = (jnp.concatenate([t[:, k * h:(k + 1) * h] for t in terms], axis=0) for k in range(2))
    (top, mid, low) = (cut3(g) for g in gram)

    def times(t, g, dot):
        r = dot(t, g[0]), dot(t[:128], g[1]), dot(t[:64], g[2])
        return (r[0][128:] + r[1][64:] + r[2]) + (r[0][64:128] + r[1][:64]) + r[0][:64]

    left = times(one, top, nn) + times(two, mid, nt)
    right = times(one, mid, nn) + times(two, low, nn)
    sk = jnp.concatenate([left, right], axis=1) * scale
    for c in range(4):
        o_ref[c * 64:(c + 1) * 64, :] = sk[:, c * 128:(c + 1) * 128]


def add_gram(blocks, cut, acc=None, test_t=None, scale=1.0):
    _, m, w = blocks[-1].shape
    args = list(blocks) + [v for v in (acc, test_t) if v is not None]
    shape = (3, 256, 256) if test_t is None else (256, 128)
    fibres = jax.ShapeDtypeStruct((16, m, w), BF16)
    return pl.pallas_call(
        lambda *r: gram_kernel(cut, scale, *r),
        in_specs=[VM] * len(args),
        out_specs=[VM] * 3,
        out_shape=[fibres, fibres, jax.ShapeDtypeStruct(shape, F32)],
        compiler_params=pltpu.CompilerParams(vmem_limit_bytes=16 << 20),
        cost_estimate=pl.CostEstimate(flops=6 * 2 * 256 * 256 * w, transcendentals=0,
                                      bytes_accessed=32 * m * w * 4),
        name="gram",
    )(*args)


def total_kernel(x_ref, o_ref):
    y = jnp.sum(x_ref[...].reshape(-1, 8, 128), axis=0)
    y = y + pltpu.roll(y, 4, 0)
    y = y + pltpu.roll(y, 2, 0)
    o_ref[...] = jnp.broadcast_to(y[None], (32, 8, 128)).reshape(256, 128)


def total(part):
    return pl.pallas_call(
        total_kernel,
        in_specs=[VM],
        out_specs=VM,
        out_shape=jax.ShapeDtypeStruct((256, 128), F32),
        compiler_params=pltpu.CompilerParams(vmem_limit_bytes=2 << 20),
        name="total",
    )(part)


def inverse_lower(aug, step):
    blocks = [aug[8 * b:8 * b + 8, :] for b in range(8)]
    sub = lax.broadcasted_iota(jnp.int32, (8, 128), 0)
    for k in range(0, 64, step):
        b0 = k // 8
        cols = [[jnp.broadcast_to(blocks[b][:, 64 + k + j:65 + k + j], (8, 128)) for b in range(b0, 8)]
                for j in range(step)]
        rows = [blocks[b0][k % 8 + j:k % 8 + j + 1, :] for j in range(step)]
        mult = []
        for j in range(step):
            r = k % 8 + j
            inv = 1.0 / cols[j][0][r:r + 1, :]
            l = [c * inv for c in cols[j]]
            l[0] = jnp.where(sub > r, l[0], 0.0)
            for j2 in range(j + 1, step):
                e = cols[j2][0][r:r + 1, :]
                cols[j2] = [c - x * e for c, x in zip(cols[j2], l)]
                rows[j2] = rows[j2] - l[0][r + j2 - j:r + j2 - j + 1, :] * rows[j]
            mult.append(l)
        for b in range(b0, 8):
            t = blocks[b]
            for j in range(step):
                t = t - mult[j][b - b0] * rows[j]
            blocks[b] = t
    lane = lax.broadcasted_iota(jnp.int32, (8, 128), 1)
    out = []
    for b in range(8):
        diag = jnp.sum(jnp.where(lane == sub + 64 + 8 * b, blocks[b], 0.0), axis=1, keepdims=True)
        out.append(blocks[b] * lax.rsqrt(diag))
    return jnp.concatenate(out, axis=0)[:, :64]


def orthonormal_t(yt, step):
    n = yt.shape[0]
    terms = cut3(yt)
    tall = jnp.concatenate(terms, axis=0)
    nine = nt(tall, jnp.concatenate([tall, jnp.zeros_like(terms[0])], axis=0))
    rows = (nine[2 * n:] + nine[n:2 * n]) + nine[:n]
    near, far = rows[:, :2 * n], rows[:, 2 * n:]
    aug = (far + pltpu.roll(far, n, 1)) + (near + pltpu.roll(near, n, 1))
    i = lax.broadcasted_iota(jnp.int32, aug.shape, 0)
    j = lax.broadcasted_iota(jnp.int32, aug.shape, 1)
    aug = jnp.where(j < n, (i == j).astype(F32), aug)
    inv = cut3(inverse_lower(aug, step))
    tall = jnp.concatenate(inv, axis=0)
    r = nn(tall, terms[0]), nn(tall[:2 * n], terms[1]), nn(tall[:n], terms[2])
    return (r[0][2 * n:] + r[1][n:] + r[2]) + (r[0][n:2 * n] + r[1][:n]) + r[0][:n]


def cells_of(x_refs, k, at):
    if k < 2:
        return x_refs[k], at
    w = x_refs[2].shape[-1]
    return (x_refs[k], at) if at < w else (x_refs[k + 2], at - w)


def core_kernel(y_ref, *refs):
    x_refs, (f_ref, o_ref) = refs[:-2], refs[-2:]
    _, _, s, w = o_ref.shape
    parts, m, _ = x_refs[0].shape
    yt = jnp.concatenate([y_ref[c * 64:(c + 1) * 64, :] for c in range(4)], axis=1)
    ft = orthonormal_t(orthonormal_t(yt, 8), 8)
    f_ref[...] = ft
    low = ft.astype(BF16)
    n = 32 * s
    i = lax.broadcasted_iota(jnp.int32, (n, 64), 0)
    j = lax.broadcasted_iota(jnp.int32, (n, 64), 1)
    wide = []
    for k in range(s):
        late = (i // 2 + k // 2) % 2
        wide.append(nn(((j == i // 8 * 4 + late * 2 + i // 4 % 2) & (i % 2 == k % 2)).astype(BF16),
                       low).astype(BF16))
    step = 512
    tile = (n // 8, 8, step)
    own = lax.broadcasted_iota(jnp.int32, tile, 1) % 4 < 2
    for c in range(w // step):
        pair = []
        for k in range(s):
            x_ref, at = cells_of(x_refs, k, c * step)
            x = x_ref[:, :, at:at + step].reshape(parts * m, step)
            t = nn(wide[k], x)
            if k % 2:
                pair[-1] = (pair[-1] + t).reshape(tile)
            else:
                pair.append(t)
        even = jnp.where(own, pair[0], pair[1])
        odd = jnp.where(own, pair[1], pair[0])
        odd = jnp.where(own, pltpu.roll(odd, 6, 1), pltpu.roll(odd, 2, 1))
        cells = slice(c * step, (c + 1) * step)
        for h, rows in enumerate((even, odd)):
            o_ref[:, 2 * h:2 * h + 2, :, cells] = rows.astype(BF16).reshape(parts, 2, s, step)


def core_blocks(full, pieces, s):
    parts, _, w = pieces[0].shape
    return pl.pallas_call(
        core_kernel,
        in_specs=[VM] * (1 + len(pieces)),
        out_specs=[VM, VM],
        out_shape=[jax.ShapeDtypeStruct((64, 512), F32),
                   jax.ShapeDtypeStruct((parts, 64 // parts, s, w), BF16)],
        compiler_params=pltpu.CompilerParams(vmem_limit_bytes=24 << 20),
        name="core",
    )(full, *pieces)


def merge_kernel(x_ref, o_ref, sem):
    parts, _, _, w = x_ref.shape
    copies = [pltpu.make_async_copy(x_ref.at[j], o_ref.at[:, :, pl.ds(j * w, w)], sem.at[j])
              for j in range(parts)]
    for c in copies:
        c.start()
    for c in copies:
        c.wait()


def merge_cells(core):
    parts, q, s, w = core.shape
    return pl.pallas_call(
        merge_kernel,
        in_specs=[VM],
        out_specs=ANY,
        out_shape=jax.ShapeDtypeStruct((q, s, parts * w), BF16),
        scratch_shapes=[pltpu.SemaphoreType.DMA((parts,))],
        compiler_params=pltpu.CompilerParams(vmem_limit_bytes=4 << 20),
        name="merge",
    )(core)


def body(fields, test_matrix):
    s, _, n = fields.shape
    parts = lax.axis_size("gx")
    w = n // parts
    axes = ("gx", "yz")
    scale = 1.0 / (s * n * lax.axis_size("yz"))
    order = ("x", "y", "x", "y")
    near = [None] * s
    near[0], near[1] = split_pair(fields[:2], parts)
    near[2], near[3] = fetch_split_pair(fields, 2, parts)
    for k in (0, 2):
        far = [[near[k + i][0]] + [None] * 3 for i in range(2)]
        for d in (1, 3, 2):
            for i in range(2):
                far[i][d] = shift(near[k + i][d], order[k + i], d)
        near[k], near[k + 1] = far
    blocks = {}
    for k in (0, 2):
        for h, sent in enumerate(regroup(near[k], near[k + 1], CUTS[k])):
            rest = [[None] * 3, [None] * 3]
            for d in (1, 3, 2):
                for i in range(2):
                    rest[i][d - 1] = shift(sent[i][d - 1], order[1 - i], d)
            blocks[k, h] = near[k] + rest[0] + near[k + 1] + rest[1]
    pieces, part = [], None
    for (k, h), block in blocks.items():
        last = (k, h) == (2, len(CUTS[2]) - 2)
        *more, part = add_gram(block, pieces_of(CUTS[k], w)[h][0], part, test_matrix.T if last else None, scale)
        pieces += more
    part = lax.all_to_all(part.reshape(128, 2, 128), axes, split_axis=0, concat_axis=0, tiled=True)
    part = total(part.reshape(256, 128))
    full = lax.all_to_all(part.reshape(128, 2, 128), axes, split_axis=0, concat_axis=0, tiled=True)
    ft, core = core_blocks(full.reshape(256, 128), pieces, s)
    core = lax.all_to_all(core, "gx", split_axis=0, concat_axis=0, tiled=True)
    return (ft.T, merge_cells(core))


def solution(mesh):
    in_specs = (P(None, "gx", "yz"), P())
    out_specs = (P(), P("gx", None, "yz"))
    return jax.shard_map(body, mesh=mesh, in_specs=in_specs, out_specs=out_specs, check_vma=False)
```

```python
import jax
import jax.numpy as jnp
from jax import lax
from jax.sharding import PartitionSpec as P
from jax.experimental import pallas as pl
from jax.experimental.pallas import tpu as pltpu

F32 = jnp.float32
CUTS = {0: (0, 8), 2: (0, 7, 8)}
BF16 = jnp.bfloat16
VM = pl.BlockSpec(memory_space=pltpu.VMEM)
ANY = pl.BlockSpec(memory_space=pl.ANY)


def nt(a, b, precision=None):
    return lax.dot_general(a, b, (((1,), (1,)), ((), ())), precision=precision,
                           preferred_element_type=F32)


def nn(a, b):
    return jnp.dot(a, b, preferred_element_type=F32)


def cut3(v):
    terms = []
    for _ in range(3):
        t = v.astype(BF16)
        terms.append(t)
        v = v - t.astype(F32)
    return terms


def place():
    g = lax.axis_index("gx")
    odd = lax.rem(lax.axis_index("yz"), 2)
    x, y = lax.rem(g, 4), lax.div(g, 4)

    def member(u, v):
        return lax.rem(u + 4, 4) * (1 + 3 * odd) + lax.rem(v + 4, 4) * (4 - 3 * odd)

    return x + odd * (y - x), y + odd * (x - y), member


def split_kernel(x_ref, *outs):
    w = outs[0].shape[-1]
    u, v, member = place()
    for k in range(2):
        for d in range(4):
            for q in range(4):
                j = member(u + q, v + d) if k else member(u + d, v + q)
                outs[4 * k + d][q] = x_ref[k, :, pl.ds(pl.multiple_of(j * w, w), w)]


def split_pair(pair, parts):
    _, m, n = pair.shape
    out = jax.ShapeDtypeStruct((4, m, n // parts), pair.dtype)
    outs = pl.pallas_call(
        split_kernel,
        in_specs=[VM],
        out_specs=[VM] * 8,
        out_shape=[out] * 8,
        compiler_params=pltpu.CompilerParams(vmem_limit_bytes=10 << 20),
        cost_estimate=pl.CostEstimate(flops=0, transcendentals=0, bytes_accessed=8 * m * n),
        name="split",
    )(pair)
    return list(outs[:4]), list(outs[4:])


def fetch_split_kernel(first, x_ref, *refs):
    outs, (buf, sem) = refs[:8], refs[8:]
    loads = [pltpu.make_async_copy(x_ref.at[first + k], buf.at[k], sem.at[k]) for k in range(2)]
    for c in loads:
        c.start()
    for c in loads:
        c.wait()
    split_kernel(buf, *outs)


def fetch_split_pair(fields, first, parts):
    _, m, n = fields.shape
    out = jax.ShapeDtypeStruct((4, m, n // parts), fields.dtype)
    outs = pl.pallas_call(
        lambda *r: fetch_split_kernel(first, *r),
        in_specs=[ANY],
        out_specs=[VM] * 8,
        out_shape=[out] * 8,
        scratch_shapes=[pltpu.VMEM((2, m, n), fields.dtype), pltpu.SemaphoreType.DMA((2,))],
        compiler_params=pltpu.CompilerParams(vmem_limit_bytes=50 << 20),
        cost_estimate=pl.CostEstimate(flops=0, transcendentals=0, bytes_accessed=8 * m * n),
        name="fetch_split",
    )(fields)
    return list(outs[:4]), list(outs[4:])


def shift(v, first, d):
    others = lax.axis_size("yz")
    pairs = []
    for g in range(16):
        for k in range(others):
            step = 1 if first == (k % 2 == 0) else 4
            c = (g // step) % 4
            t = g + ((c + d) % 4 - c) * step
            pairs.append((g * others + k, t * others + k))
    return lax.ppermute(v, ("gx", "yz"), pairs)


def pieces_of(cuts, w):
    return [(p * w // 8, q * w // 8) for p, q in zip(cuts, cuts[1:])]


def regroup_kernel(cuts, *refs):
    outs = list(refs[8:])
    for k in range(2):
        got = refs[4 * k:4 * k + 4]
        for lo, hi in pieces_of(cuts, got[0].shape[-1]):
            for q in range(1, 4):
                out = outs.pop(0)
                for d in range(4):
                    out[d] = got[d][q, :, lo:hi]


def regroup(one, two, cuts):
    n, m, w = one[0].shape
    count = len(cuts) - 1
    shapes = [jax.ShapeDtypeStruct((n, m, hi - lo), one[0].dtype)
              for lo, hi in pieces_of(cuts, w) for _ in range(3)]
    outs = pl.pallas_call(
        lambda *r: regroup_kernel(cuts, *r),
        in_specs=[VM] * 8,
        out_specs=[VM] * (6 * count),
        out_shape=shapes * 2,
        compiler_params=pltpu.CompilerParams(vmem_limit_bytes=6 << 20),
        cost_estimate=pl.CostEstimate(flops=0, transcendentals=0, bytes_accessed=4 * one[0].size),
        name="regroup",
    )(*one, *two)
    return [[outs[3 * (count * k + h):3 * (count * k + h) + 3] for k in range(2)] for h in range(count)]


def gram_kernel(cut, scale, *refs):
    blocks, rest = (refs[:7], refs[7:14]), list(refs[14:])
    acc = rest.pop(0) if len(rest) > 3 else None
    t_ref = rest.pop(0) if len(rest) > 3 else None
    p_refs, o_ref = rest[:2], rest[2]
    parts, m, w = p_refs[0].shape
    u, v, member = place()
    h = parts * m // 2
    gram = None if acc is None else [acc[k] for k in range(3)]
    for k in range(2):
        for d1 in range(4):
            for d2 in range(4):
                g = member(u - d2, v - d1) if k else member(u - d1, v - d2)
                if d2 == 0:
                    p_refs[k][g] = blocks[k][d1][0, :, cut:cut + w]
                else:
                    p_refs[k][g] = blocks[k][3 + d2][d1]
    for k in range(2):
        top = p_refs[k][:parts // 2].reshape(h, w)
        low = p_refs[k][parts // 2:].reshape(h, w)
        more = [nt(p, q) for p, q in ((top, top), (top, low), (low, low))]
        gram = more if gram is None else [p + q for p, q in zip(gram, more)]
    if t_ref is None:
        for k in range(3):
            o_ref[k] = gram[k]
        return
    terms = cut3(t_ref[...])
    one, two = (jnp.concatenate([t[:, k * h:(k + 1) * h] for t in terms], axis=0) for k in range(2))
    (top, mid, low) = (cut3(g) for g in gram)

    def times(t, g, dot):
        r = dot(t, g[0]), dot(t[:128], g[1]), dot(t[:64], g[2])
        return (r[0][128:] + r[1][64:] + r[2]) + (r[0][64:128] + r[1][:64]) + r[0][:64]

    left = times(one, top, nn) + times(two, mid, nt)
    right = times(one, mid, nn) + times(two, low, nn)
    sk = jnp.concatenate([left, right], axis=1) * scale
    for c in range(4):
        o_ref[c * 64:(c + 1) * 64, :] = sk[:, c * 128:(c + 1) * 128]


def add_gram(blocks, cut, acc=None, test_t=None, scale=1.0):
    _, m, w = blocks[-1].shape
    args = list(blocks) + [v for v in (acc, test_t) if v is not None]
    shape = (3, 256, 256) if test_t is None else (256, 128)
    fibres = jax.ShapeDtypeStruct((16, m, w), BF16)
    return pl.pallas_call(
        lambda *r: gram_kernel(cut, scale, *r),
        in_specs=[VM] * len(args),
        out_specs=[VM] * 3,
        out_shape=[fibres, fibres, jax.ShapeDtypeStruct(shape, F32)],
        compiler_params=pltpu.CompilerParams(vmem_limit_bytes=16 << 20),
        cost_estimate=pl.CostEstimate(flops=6 * 2 * 256 * 256 * w, transcendentals=0,
                                      bytes_accessed=32 * m * w * 4),
        name="gram",
    )(*args)


def total_kernel(x_ref, o_ref):
    y = jnp.sum(x_ref[...].reshape(-1, 8, 128), axis=0)
    y = y + pltpu.roll(y, 4, 0)
    y = y + pltpu.roll(y, 2, 0)
    o_ref[...] = jnp.broadcast_to(y[None], (32, 8, 128)).reshape(256, 128)


def total(part):
    return pl.pallas_call(
        total_kernel,
        in_specs=[VM],
        out_specs=VM,
        out_shape=jax.ShapeDtypeStruct((256, 128), F32),
        compiler_params=pltpu.CompilerParams(vmem_limit_bytes=2 << 20),
        name="total",
    )(part)


def inverse_lower(aug, step):
    blocks = [aug[8 * b:8 * b + 8, :] for b in range(8)]
    sub = lax.broadcasted_iota(jnp.int32, (8, 128), 0)
    for k in range(0, 64, step):
        b0 = k // 8
        cols = [[jnp.broadcast_to(blocks[b][:, 64 + k + j:65 + k + j], (8, 128)) for b in range(b0, 8)]
                for j in range(step)]
        rows = [blocks[b0][k % 8 + j:k % 8 + j + 1, :] for j in range(step)]
        mult = []
        for j in range(step):
            r = k % 8 + j
            inv = 1.0 / cols[j][0][r:r + 1, :]
            l = [c * inv for c in cols[j]]
            l[0] = jnp.where(sub > r, l[0], 0.0)
            for j2 in range(j + 1, step):
                e = cols[j2][0][r:r + 1, :]
                cols[j2] = [c - x * e for c, x in zip(cols[j2], l)]
                rows[j2] = rows[j2] - l[0][r + j2 - j:r + j2 - j + 1, :] * rows[j]
            mult.append(l)
        for b in range(b0, 8):
            t = blocks[b]
            for j in range(step):
                t = t - mult[j][b - b0] * rows[j]
            blocks[b] = t
    lane = lax.broadcasted_iota(jnp.int32, (8, 128), 1)
    out = []
    for b in range(8):
        diag = jnp.sum(jnp.where(lane == sub + 64 + 8 * b, blocks[b], 0.0), axis=1, keepdims=True)
        out.append(blocks[b] * lax.rsqrt(diag))
    return jnp.concatenate(out, axis=0)[:, :64]


def orthonormal_t(yt, step):
    n = yt.shape[0]
    terms = cut3(yt)
    tall = jnp.concatenate(terms, axis=0)
    nine = nt(tall, jnp.concatenate([tall, jnp.zeros_like(terms[0])], axis=0))
    rows = (nine[2 * n:] + nine[n:2 * n]) + nine[:n]
    near, far = rows[:, :2 * n], rows[:, 2 * n:]
    aug = (far + pltpu.roll(far, n, 1)) + (near + pltpu.roll(near, n, 1))
    i = lax.broadcasted_iota(jnp.int32, aug.shape, 0)
    j = lax.broadcasted_iota(jnp.int32, aug.shape, 1)
    aug = jnp.where(j < n, (i == j).astype(F32), aug)
    inv = cut3(inverse_lower(aug, step))
    tall = jnp.concatenate(inv, axis=0)
    r = nn(tall, terms[0]), nn(tall[:2 * n], terms[1]), nn(tall[:n], terms[2])
    return (r[0][2 * n:] + r[1][n:] + r[2]) + (r[0][n:2 * n] + r[1][:n]) + r[0][:n]


def cells_of(x_refs, k, at):
    if k < 2:
        return x_refs[k], at
    w = x_refs[2].shape[-1]
    return (x_refs[k], at) if at < w else (x_refs[k + 2], at - w)


def core_kernel(y_ref, *refs):
    x_refs, (f_ref, o_ref, buf, sem) = refs[:-4], refs[-4:]
    _, _, s, w = o_ref.shape
    parts, m, _ = x_refs[0].shape
    yt = jnp.concatenate([y_ref[c * 64:(c + 1) * 64, :] for c in range(4)], axis=1)
    ft = orthonormal_t(orthonormal_t(yt, 8), 8)
    buf[...] = ft
    low = ft.astype(BF16)
    n = 32 * s
    i = lax.broadcasted_iota(jnp.int32, (n, 64), 0)
    j = lax.broadcasted_iota(jnp.int32, (n, 64), 1)
    wide = []
    for k in range(s):
        late = (i // 2 + k // 2) % 2
        wide.append(nn(((j == i // 8 * 4 + late * 2 + i // 4 % 2) & (i % 2 == k % 2)).astype(BF16),
                       low).astype(BF16))
    step = 256
    tile = (n // 8, 8, step)
    own = lax.broadcasted_iota(jnp.int32, tile, 1) % 4 < 2
    for c in range(w // step):
        pair = []
        for k in range(s):
            x_ref, at = cells_of(x_refs, k, c * step)
            x = x_ref[:, :, at:at + step].reshape(parts * m, step)
            t = nn(wide[k], x)
            if k % 2:
                pair[-1] = (pair[-1] + t).reshape(tile)
            else:
                pair.append(t)
        even = jnp.where(own, pair[0], pair[1])
        odd = jnp.where(own, pair[1], pair[0])
        odd = jnp.where(own, pltpu.roll(odd, 6, 1), pltpu.roll(odd, 2, 1))
        cells = slice(c * step, (c + 1) * step)
        for h, rows in enumerate((even, odd)):
            o_ref[:, 2 * h:2 * h + 2, :, cells] = rows.astype(BF16).reshape(parts, 2, s, step)
        if c == 0:
            pltpu.make_async_copy(buf, f_ref, sem).start()
    pltpu.make_async_copy(buf, f_ref, sem).wait()


def core_blocks(full, pieces, s):
    parts, _, w = pieces[0].shape
    return pl.pallas_call(
        core_kernel,
        in_specs=[VM] * (1 + len(pieces)),
        out_specs=[ANY, VM],
        out_shape=[jax.ShapeDtypeStruct((64, 512), F32),
                   jax.ShapeDtypeStruct((parts, 64 // parts, s, w), BF16)],
        scratch_shapes=[pltpu.VMEM((64, 512), F32), pltpu.SemaphoreType.DMA],
        compiler_params=pltpu.CompilerParams(vmem_limit_bytes=24 << 20),
        name="core",
    )(full, *pieces)


def merge_kernel(x_ref, o_ref, sem):
    parts, _, _, w = x_ref.shape
    copies = [pltpu.make_async_copy(x_ref.at[j], o_ref.at[:, :, pl.ds(j * w, w)], sem.at[j])
              for j in range(parts)]
    for c in copies:
        c.start()
    for c in copies:
        c.wait()


def merge_cells(core):
    parts, q, s, w = core.shape
    return pl.pallas_call(
        merge_kernel,
        in_specs=[VM],
        out_specs=ANY,
        out_shape=jax.ShapeDtypeStruct((q, s, parts * w), BF16),
        scratch_shapes=[pltpu.SemaphoreType.DMA((parts,))],
        compiler_params=pltpu.CompilerParams(vmem_limit_bytes=4 << 20),
        name="merge",
    )(core)


def body(fields, test_matrix):
    s, _, n = fields.shape
    parts = lax.axis_size("gx")
    w = n // parts
    axes = ("gx", "yz")
    scale = 1.0 / (s * n * lax.axis_size("yz"))
    near = [None] * s
    near[0], near[1] = split_pair(fields[:2], parts)
    near[2], near[3] = fetch_split_pair(fields, 2, parts)
    for k in (0, 2):
        far = [[near[k + i][0]] + [None] * 3 for i in range(2)]
        for d in (1, 3, 2):
            for i in range(2):
                far[i][d] = shift(near[k + i][d], i == 0, d)
        near[k], near[k + 1] = far
    blocks = {}
    for k in (0, 2):
        for h, sent in enumerate(regroup(near[k], near[k + 1], CUTS[k])):
            rest = [[None] * 3, [None] * 3]
            for d in (2, 1, 3) if k else (1, 3, 2):
                for i in range(2):
                    rest[i][d - 1] = shift(sent[i][d - 1], i == 1, d)
            blocks[k, h] = near[k] + rest[0] + near[k + 1] + rest[1]
    pieces, part = [], None
    for (k, h), block in blocks.items():
        last = (k, h) == (2, len(CUTS[2]) - 2)
        *more, part = add_gram(block, pieces_of(CUTS[k], w)[h][0], part, test_matrix.T if last else None, scale)
        pieces += more
    part = lax.all_to_all(part.reshape(128, 2, 128), axes, split_axis=0, concat_axis=0, tiled=True)
    part = total(part.reshape(256, 128))
    full = lax.all_to_all(part.reshape(128, 2, 128), axes, split_axis=0, concat_axis=0, tiled=True)
    ft, core = core_blocks(full.reshape(256, 128), pieces, s)
    core = lax.all_to_all(core, "gx", split_axis=0, concat_axis=0, tiled=True)
    return (ft.T, merge_cells(core))


def solution(mesh):
    in_specs = (P(None, "gx", "yz"), P())
    out_specs = (P(), P("gx", None, "yz"))
    return jax.shard_map(body, mesh=mesh, in_specs=in_specs, out_specs=out_specs, check_vma=False)
```
